32 devices in a mesh: ctx: 8 (over y, x, core), wt: 4 (over z).
Axes of the slice: x: 2, y: 2, z: 4, core: 2. Of those that a mesh axis runs over, the one named last changes fastest.
Arguments:
- block_in: float32 [4, 1024, 896], P('wt', 'ctx'), may hold values from -6 to 6
- cotangent: float32 [4, 1024, 896], P('wt', 'ctx'), may hold values from -12 to 12
- pairs: int32 [8], replicated, may hold values from 0 to 7, as said below
- positions: int32 [4, 1024], P('wt', 'ctx'), may hold values from 0 to 1023, as said below
- params: float32 [4, 3728096], P('wt'), may hold values from -16 to 16
- moment1: float32 [4, 3728096], P('wt', 'ctx'), may hold values from -100000 to 100000
- moment2: float32 [4, 3728096], P('wt', 'ctx'), may hold values from 0 to 10000000000, as said below
Outputs:
- block_out: float32 [4, 1024, 896], P('wt', 'ctx')
- input_grad: float32 [4, 1024, 896], P('wt', 'ctx')
- param_grad: float32 [4, 3728096], P('wt', 'ctx')
- new_params: float32 [4, 3728096], P('wt', 'ctx')
- new_moment1: float32 [4, 3728096], P('wt', 'ctx')
- new_moment2: float32 [4, 3728096], P('wt', 'ctx')
The draws below stay inside these ranges and needn't reach their ends.
Inputs may be any that keep to these rules, and one draw needn't show every extreme that they name: a permutation of 0 to 7; context index c holds blocks pairs[c] and 15 - pairs[c] of 64 tokens of every sequence. positions equals order, the causal position that pairs gives each row. `moment2`: positive.
All inputs are finite; a program needn't handle non-finite values.
Results may differ from the reference program's by a relative error of at most 0.012.
The reference program's roundings to bfloat16 on the way count: a program that leaves them out, or rounds other values in their place, can miss the bound.
Values may be sent and summed in bfloat16 or wider, within the bound.
A program may use at most 256 MiB of HBM per device.

```python
import math
import jax
import jax.numpy as jnp
from jax import lax

D = 896
QUERY_HEADS = 14
KEY_VALUE_HEADS = 2
HEAD_SIZE = 64
FF = 4864
TOK_DEV = 128
QW = 896
KEY_FEATURES = 128
HALF = 64
SEQUENCE_TOKENS = 1024
SHARD = 3728096
N_CTX = 8
N_WT = 4


def mirror_pairs(key):
    return jax.random.permutation(jax.random.fold_in(key, 11), N_CTX).astype(jnp.int32)


def draw_pairs(key, part):
    return mirror_pairs(key)


def draw_positions(key, part):
    chosen_pairs = mirror_pairs(key)
    row_ids = jnp.arange(SEQUENCE_TOKENS, dtype=jnp.int32)
    ctx_ids = row_ids // TOK_DEV
    local_row = row_ids % TOK_DEV
    chosen = jnp.sum(jnp.where(ctx_ids[:, None] == jnp.arange(N_CTX, dtype=jnp.int32)[None, :], chosen_pairs[None, :], 0), 1)
    block_id = jnp.where(local_row < HALF, chosen, 2 * N_CTX - 1 - chosen)
    order = (block_id * HALF + local_row % HALF).astype(jnp.int32)
    return jnp.broadcast_to(order[None, :], (N_WT, SEQUENCE_TOKENS)).astype(jnp.int32)


def draw_cotangent(key, part):
    noise = jax.random.truncated_normal(jax.random.fold_in(key, 51), -4.0, 4.0, (N_WT, SEQUENCE_TOKENS, D), jnp.float32)
    ratio_log = math.log(3.0)
    spread_pos = jnp.arange(N_WT, dtype=jnp.float32) / max(N_WT - 1, 1) - 0.5
    seq_scale = jnp.exp(ratio_log * spread_pos)
    return noise * seq_scale[:, None, None]


def shard_bounds_drawn():
    shapes = [(D, 0), (D, QW), (QW, 0), (D, KEY_FEATURES), (KEY_FEATURES, 0), (D, KEY_FEATURES), (KEY_FEATURES, 0), (QW, D), (D, 0), (FF, D), (FF, D), (FF, D)]
    bounds = [0]
    for rows_full, cols in shapes:
        length = rows_full // N_WT
        if cols > 0:
            length = length * cols
        bounds.append(bounds[-1] + length)
    return bounds


def layout_ids():
    bounds = shard_bounds_drawn()
    column = jnp.arange(SHARD, dtype=jnp.int32)
    segment = jnp.zeros((SHARD,), jnp.int32)
    for bound in bounds[1:12]:
        segment = segment + (column >= bound).astype(jnp.int32)
    return jnp.broadcast_to(segment[None, :], (N_WT, SHARD))


def pick_scale(segment, table):
    result = jnp.zeros(segment.shape, jnp.float32)
    for number in range(12):
        result = result + jnp.where(segment == number, table[number], 0.0)
    return result


def grad_scales():
    factor = math.sqrt(N_WT * SEQUENCE_TOKENS / 16384.0)
    return [15.0 * factor, 12.0 * factor, 12.0 * factor, 12.0 * factor, 12.0 * factor, 16.0 * factor, 800.0 * factor, 8.0 * factor, 40.0 * factor, 25.0 * factor, 20.0 * factor, 50.0 * factor]


def draw_params(key, part):
    segment = layout_ids()
    noise = jax.random.truncated_normal(jax.random.fold_in(key, 21), -4.0, 4.0, (N_WT, SHARD), jnp.float32)
    spreads = [0.1, 1.0 / math.sqrt(D), 0.08, 1.0 / math.sqrt(D), 0.08, 1.0 / math.sqrt(D), 0.05, 1.0 / math.sqrt(2 * HEAD_SIZE), 0.1, 1.0 / math.sqrt(D), 1.0 / math.sqrt(D), 1.0 / math.sqrt(FF)]
    values = noise * pick_scale(segment, spreads)
    is_gain = (segment == 0) | (segment == 8)
    return jnp.where(is_gain, 1.0 + values, values)


def draw_moment1(key, part):
    segment = layout_ids()
    noise = jax.random.truncated_normal(jax.random.fold_in(key, 31), -4.0, 4.0, (N_WT, SHARD), jnp.float32)
    return noise * 0.1 * pick_scale(segment, grad_scales())


def draw_moment2(key, part):
    segment = layout_ids()
    level = jax.random.uniform(jax.random.fold_in(key, 41), (N_WT, SHARD), jnp.float32, math.log(0.05), math.log(0.2))
    base = pick_scale(segment, grad_scales())
    return jnp.exp(level) * base * base


def levels(rng, extent, shards, low, top_value):
    def one(axis_at, blocks):
        steps = jax.random.uniform(jax.random.fold_in(jax.random.fold_in(rng, 6), axis_at), (blocks,), jnp.float32, low / len(shards), top_value / len(shards))
        return jnp.repeat(jnp.exp(steps), extent[axis_at] // blocks).reshape((-1,) + (1,) * (len(extent) - axis_at - 1))

    level = one(*shards[0])
    for cut in shards[1:]:
        level = level * one(*cut)
    return level


def centred(stream_key, extent, width, most, cuts=(), kind=jnp.bfloat16):
    level = levels(stream_key, extent, cuts, -0.22, 0.18) if cuts else 1.0
    entries = jax.random.normal(stream_key, extent, jnp.float32) * width * level
    return jnp.minimum(jnp.maximum(entries, -most), most).astype(kind)


def setup_inputs(seed: int = 0) -> dict:
    streams_of = jax.random.split(jax.random.key(seed), 8)
    block_in = centred(streams_of[0], (N_WT, SEQUENCE_TOKENS, D), 1.0, 6.0, ((0, 4), (1, 8)), jnp.float32)
    cotangent = draw_cotangent(jax.random.fold_in(streams_of[7], 71), 0)
    pairs = draw_pairs(jax.random.fold_in(streams_of[7], 71), 0)
    positions = draw_positions(jax.random.fold_in(streams_of[7], 71), 0)
    params = draw_params(jax.random.fold_in(streams_of[7], 71), 0)
    moment1 = draw_moment1(jax.random.fold_in(streams_of[7], 71), 0)
    moment2 = draw_moment2(jax.random.fold_in(streams_of[7], 71), 0)
    return dict(block_in=block_in, cotangent=cotangent, pairs=pairs, positions=positions, params=params, moment1=moment1, moment2=moment2)


theta_base = 1000000.0
norm_eps = 1e-06
beta_one = 0.9
beta_two = 0.95
adam_eps = 1e-08
learn_rate = 0.02
decay_rate = 0.1
step_count = 10.0

def piece_shapes():
    return [(D, 0), (D, QW), (QW, 0), (D, KEY_FEATURES), (KEY_FEATURES, 0), (D, KEY_FEATURES), (KEY_FEATURES, 0), (QW, D), (D, 0), (FF, D), (FF, D), (FF, D)]

def shard_bounds(parts):
    bounds = [0]
    for rows_full, cols in piece_shapes():
        length = rows_full // parts
        if cols > 0:
            length = length * cols
        bounds.append(bounds[-1] + length)
    return bounds

def unpack(rows_arr, parts, first, last):
    bounds = shard_bounds(parts)
    shapes = piece_shapes()
    count = rows_arr.shape[0]
    base = bounds[first]
    result = []
    for number in range(first, last):
        rows_full, cols = shapes[number]
        piece = rows_arr[:, bounds[number] - base:bounds[number + 1] - base]
        if cols > 0:
            result.append(piece.reshape(count * (rows_full // parts), cols))
        else:
            result.append(piece.reshape(-1))
    return result

def pack(pieces, parts):
    return jnp.concatenate([piece.reshape(parts, -1) for piece in pieces], 1)

def decay_mask(index_vec, parts):
    bounds = shard_bounds(parts)
    result = jnp.zeros(index_vec.shape, jnp.float32)
    for number in (1, 3, 5, 7, 9, 10, 11):
        inside = (index_vec >= bounds[number]) & (index_vec < bounds[number + 1])
        result = result + jnp.where(inside, 1.0, 0.0).astype(jnp.float32)
    return result

def rope_tables(position):
    freq_index = jnp.arange(HEAD_SIZE // 2, dtype=jnp.float32)
    inverse = jnp.exp(freq_index * (-2.0 * math.log(theta_base) / HEAD_SIZE))
    angles = position.astype(jnp.float32)[:, None] * inverse[None, :]
    cosine_table = jnp.cos(angles)
    sine_lookup = jnp.sin(angles)
    return (jnp.concatenate([cosine_table, cosine_table], 1), jnp.concatenate([sine_lookup, sine_lookup], 1))

def rotary_apply(values, cosine_table, sine_lookup):
    top_half = values[..., HEAD_SIZE // 2:]
    low_half = values[..., :HEAD_SIZE // 2]
    turned = jnp.concatenate([-top_half, low_half], -1)
    return values * cosine_table[:, None, :] + turned * sine_lookup[:, None, :]

def rotary_inverse(gradient, cosine_table, sine_lookup):
    scaled = gradient * sine_lookup[:, None, :]
    turned = jnp.concatenate([scaled[..., HEAD_SIZE // 2:], -scaled[..., :HEAD_SIZE // 2]], -1)
    return gradient * cosine_table[:, None, :] + turned

def causal_order(pairs):
    row_ids = jnp.arange(SEQUENCE_TOKENS, dtype=jnp.int32)
    ctx_ids = row_ids // TOK_DEV
    local_row = row_ids % TOK_DEV
    chosen = lax.optimization_barrier(jnp.sum(jnp.where(ctx_ids[:, None] == jnp.arange(N_CTX, dtype=jnp.int32)[None, :], pairs[None, :], 0), 1))
    block_id = jnp.where(local_row < HALF, chosen, 2 * N_CTX - 1 - chosen)
    return (block_id * HALF + local_row % HALF).astype(jnp.int32)

def outer_dot(left, right):
    return lax.dot_general(left, right, (((0,), (0,)), ((), ())), preferred_element_type=jnp.float32)

def inner_dot(left, right):
    return lax.dot_general(left, right, (((1,), (1,)), ((), ())), preferred_element_type=jnp.float32)

def feed_forward(mid_rows, cot_rows, gain_two, wg_b, wu_b, wd_b):
    gain_full = gain_two.astype(jnp.float32)
    inv_rms = lax.rsqrt(lax.optimization_barrier(jnp.mean(mid_rows * mid_rows, -1, keepdims=True)) + norm_eps)
    normed = (mid_rows * inv_rms * gain_full).astype(jnp.bfloat16)
    gate_pre = inner_dot(normed, wg_b)
    up_pre = inner_dot(normed, wu_b)
    sigmoid_gate = jax.nn.sigmoid(gate_pre)
    silu_gate = gate_pre * sigmoid_gate
    hidden_bf = (silu_gate * up_pre).astype(jnp.bfloat16)
    out_rows = mid_rows + jnp.dot(hidden_bf, wd_b, preferred_element_type=jnp.float32)
    cot_bf = cot_rows.astype(jnp.bfloat16)
    grad_wd = outer_dot(hidden_bf, cot_bf)
    d_hidden = inner_dot(cot_bf, wd_b)
    d_gate = (d_hidden * up_pre * sigmoid_gate * (1.0 + gate_pre * (1.0 - sigmoid_gate))).astype(jnp.bfloat16)
    d_up = (d_hidden * silu_gate).astype(jnp.bfloat16)
    grad_wg = outer_dot(d_gate, normed)
    grad_wu = outer_dot(d_up, normed)
    d_norm = jnp.dot(d_gate, wg_b, preferred_element_type=jnp.float32) + jnp.dot(d_up, wu_b, preferred_element_type=jnp.float32)
    grad_gain = lax.optimization_barrier(jnp.sum(d_norm * mid_rows * inv_rms, 0))
    d_scaled = d_norm * gain_full
    d_mid = cot_rows + inv_rms * d_scaled - mid_rows * (inv_rms * inv_rms * inv_rms) * lax.optimization_barrier(jnp.mean(d_scaled * mid_rows, -1, keepdims=True))
    return (out_rows, d_mid, grad_gain, grad_wg, grad_wu, grad_wd)

def reference(block_in, cotangent, pairs, positions, params, moment1, moment2):
    group = QUERY_HEADS // KEY_VALUE_HEADS
    score_scale = 1.0 / math.sqrt(HEAD_SIZE)
    all_rows = N_WT * SEQUENCE_TOKENS
    gain_b, wq_b, bq_b, wk_b, bk_b, wv_b, bv_b, wo_b, gain_two, wg_b, wu_b, wd_b = unpack(params.astype(jnp.bfloat16), N_WT, 0, 12)
    order_pos = causal_order(pairs)
    inverse_order = jnp.zeros((SEQUENCE_TOKENS,), jnp.int32).at[order_pos].set(jnp.arange(SEQUENCE_TOKENS, dtype=jnp.int32))
    x_rows = block_in[:, inverse_order].reshape(all_rows, D)
    cot_rows = cotangent[:, inverse_order].reshape(all_rows, D)
    rope_pos = positions[:, inverse_order].reshape(all_rows)
    gain_full = gain_b.astype(jnp.float32)
    inv_rms = lax.rsqrt(lax.optimization_barrier(jnp.mean(x_rows * x_rows, -1, keepdims=True)) + norm_eps)
    normed = (x_rows * inv_rms * gain_full).astype(jnp.bfloat16)
    queries = jnp.dot(normed, wq_b, preferred_element_type=jnp.float32) + bq_b.astype(jnp.float32)
    key_projected = jnp.dot(normed, wk_b, preferred_element_type=jnp.float32) + bk_b.astype(jnp.float32)
    value_projected = jnp.dot(normed, wv_b, preferred_element_type=jnp.float32) + bv_b.astype(jnp.float32)
    cosine_table, sine_lookup = rope_tables(rope_pos)
    query_narrow = rotary_apply(queries.reshape(all_rows, QUERY_HEADS, HEAD_SIZE), cosine_table, sine_lookup).astype(jnp.bfloat16)
    key_narrow = rotary_apply(key_projected.reshape(all_rows, KEY_VALUE_HEADS, HEAD_SIZE), cosine_table, sine_lookup).astype(jnp.bfloat16)
    value_narrow = value_projected.astype(jnp.bfloat16).reshape(all_rows, KEY_VALUE_HEADS, HEAD_SIZE)
    query_block = min(512, SEQUENCE_TOKENS)
    block_count = SEQUENCE_TOKENS // query_block
    query_wide = query_narrow.astype(jnp.float32).reshape(N_WT, block_count, query_block, KEY_VALUE_HEADS, group, HEAD_SIZE)
    k_float = key_narrow.astype(jnp.float32).reshape(N_WT, SEQUENCE_TOKENS, KEY_VALUE_HEADS, HEAD_SIZE)
    v_float = value_narrow.astype(jnp.float32).reshape(N_WT, SEQUENCE_TOKENS, KEY_VALUE_HEADS, HEAD_SIZE)
    start_offsets = jnp.arange(block_count, dtype=jnp.int32) * query_block
    key_ids = jnp.arange(SEQUENCE_TOKENS, dtype=jnp.int32)

    def block_scores(q_part, k_seq, start_row):
        scores = score_scale * jnp.einsum('qkgd,tkd->kgqt', q_part, k_seq)
        query_ids = start_row + jnp.arange(query_block, dtype=jnp.int32)
        visible = key_ids[None, :] <= query_ids[:, None]
        return (jnp.where(visible, scores, -jnp.inf), visible)

    def forward_sequence(inputs):
        q_seq, k_seq, v_seq = inputs

        def forward_block(block_inputs):
            q_part, start_row = block_inputs
            scores, visible = block_scores(q_part, k_seq, start_row)
            peak = lax.optimization_barrier(jnp.max(scores, -1, keepdims=True))
            log_sum = peak + jnp.log(lax.optimization_barrier(jnp.sum(jnp.exp(scores - peak), -1, keepdims=True)))
            probs_bf = jnp.where(visible, jnp.exp(scores - log_sum), 0.0).astype(jnp.bfloat16)
            context_part = jnp.einsum('kgqt,tkd->qkgd', probs_bf.astype(jnp.float32), v_seq)
            return (context_part, log_sum)
        return lax.map(forward_block, (q_seq, start_offsets))
    full_context, full_log_sum = lax.map(forward_sequence, (query_wide, k_float, v_float))
    context_rows = full_context.reshape(all_rows, QW)
    context_bf = context_rows.astype(jnp.bfloat16)
    mid_rows = x_rows + jnp.dot(context_bf, wo_b, preferred_element_type=jnp.float32)
    ff_rows = math.gcd(all_rows, 4096)
    ff_count = all_rows // ff_rows

    def ff_step(carry, inputs):
        mid_part, cot_part = inputs
        out_part, dmid_part, g_part, wg_part, wu_part, wd_part = feed_forward(mid_part, cot_part, gain_two, wg_b, wu_b, wd_b)
        carry = (carry[0] + g_part, carry[1] + wg_part, carry[2] + wu_part, carry[3] + wd_part)
        return (carry, (out_part, dmid_part))
    ff_init = (jnp.zeros((D,), jnp.float32), jnp.zeros((FF, D), jnp.float32), jnp.zeros((FF, D), jnp.float32), jnp.zeros((FF, D), jnp.float32))
    ff_sums, (out_blocks, dmid_blocks) = lax.scan(ff_step, ff_init, (mid_rows.reshape(ff_count, ff_rows, D), cot_rows.reshape(ff_count, ff_rows, D)))
    grad_gain_two, grad_wg, grad_wu, grad_wd = ff_sums
    out_rows = out_blocks.reshape(all_rows, D)
    d_mid = dmid_blocks.reshape(all_rows, D)
    d_mid_bf = d_mid.astype(jnp.bfloat16)
    grad_wo = outer_dot(context_bf, d_mid_bf)
    context_gradient = inner_dot(d_mid_bf, wo_b)
    context_gradient_narrow = context_gradient.astype(jnp.bfloat16)
    delta_rows = lax.optimization_barrier(jnp.sum((context_gradient * context_rows).reshape(all_rows, KEY_VALUE_HEADS, group, HEAD_SIZE), -1))
    gradient_wide = context_gradient_narrow.astype(jnp.float32).reshape(N_WT, block_count, query_block, KEY_VALUE_HEADS, group, HEAD_SIZE)
    block_deltas = delta_rows.reshape(N_WT, block_count, query_block, KEY_VALUE_HEADS, group)

    def backward_sequence(inputs):
        q_seq, g_seq, lse_seq, delta_seq, k_seq, v_seq = inputs

        def backward_block(carry, block_inputs):
            key_acc, value_acc = carry
            q_part, d_part, lse_part, delta_part, start_row = block_inputs
            scores, visible = block_scores(q_part, k_seq, start_row)
            probs = jnp.where(visible, jnp.exp(scores - lse_part), 0.0)
            probs_bf = probs.astype(jnp.bfloat16).astype(jnp.float32)
            d_probs = jnp.einsum('qkgd,tkd->kgqt', d_part, v_seq)
            delta_t = jnp.transpose(delta_part, (1, 2, 0))[..., None]
            d_scores = (probs * (d_probs - delta_t)).astype(jnp.bfloat16).astype(jnp.float32)
            d_query = score_scale * jnp.einsum('kgqt,tkd->qkgd', d_scores, k_seq)
            key_acc = key_acc + score_scale * jnp.einsum('kgqt,qkgd->tkd', d_scores, q_part)
            value_acc = value_acc + jnp.einsum('kgqt,qkgd->tkd', probs_bf, d_part)
            return ((key_acc, value_acc), d_query)
        empty_rows = jnp.zeros((SEQUENCE_TOKENS, KEY_VALUE_HEADS, HEAD_SIZE), jnp.float32)
        (key_acc, value_acc), d_query = lax.scan(backward_block, (empty_rows, empty_rows), (q_seq, g_seq, lse_seq, delta_seq, start_offsets))
        return (d_query, key_acc, value_acc)
    query_blocks, rotated_keys, value_sums = lax.map(backward_sequence, (query_wide, gradient_wide, full_log_sum, block_deltas, k_float, v_float))
    d_query = rotary_inverse(query_blocks.reshape(all_rows, QUERY_HEADS, HEAD_SIZE), cosine_table, sine_lookup).reshape(all_rows, QW)
    key_gradient = rotary_inverse(rotated_keys.reshape(all_rows, KEY_VALUE_HEADS, HEAD_SIZE), cosine_table, sine_lookup).reshape(all_rows, KEY_FEATURES)
    value_gradient = value_sums.reshape(all_rows, KEY_FEATURES)
    dq_bf = d_query.astype(jnp.bfloat16)
    dk_bf = key_gradient.astype(jnp.bfloat16)
    dv_bf = value_gradient.astype(jnp.bfloat16)
    grad_wq = outer_dot(normed, dq_bf)
    grad_wk = outer_dot(normed, dk_bf)
    grad_wv = outer_dot(normed, dv_bf)
    d_norm = inner_dot(dq_bf, wq_b) + inner_dot(dk_bf, wk_b) + inner_dot(dv_bf, wv_b)
    grad_gain = lax.optimization_barrier(jnp.sum(d_norm * x_rows * inv_rms, 0))
    d_scaled = d_norm * gain_full
    d_input = inv_rms * d_scaled - x_rows * (inv_rms * inv_rms * inv_rms) * lax.optimization_barrier(jnp.mean(d_scaled * x_rows, -1, keepdims=True))
    grad_rows = d_mid + d_input
    param_grad = pack([grad_gain, grad_wq, lax.optimization_barrier(jnp.sum(dq_bf.astype(jnp.float32), 0)), grad_wk, lax.optimization_barrier(jnp.sum(dk_bf.astype(jnp.float32), 0)), grad_wv, lax.optimization_barrier(jnp.sum(dv_bf.astype(jnp.float32), 0)), grad_wo, grad_gain_two, grad_wg, grad_wu, grad_wd], N_WT)
    new_moment1 = beta_one * moment1 + (1.0 - beta_one) * param_grad
    new_moment2 = beta_two * moment2 + (1.0 - beta_two) * param_grad * param_grad
    m_hat = new_moment1 / (1.0 - beta_one ** step_count)
    v_hat = new_moment2 / (1.0 - beta_two ** step_count)
    decay = decay_mask(jnp.arange(SHARD, dtype=jnp.int32), N_WT)[None, :]
    new_params = params - learn_rate * (m_hat / (jnp.sqrt(v_hat) + adam_eps) + decay_rate * decay * params)
    block_out = out_rows.reshape(N_WT, SEQUENCE_TOKENS, D)[:, order_pos]
    input_grad = grad_rows.reshape(N_WT, SEQUENCE_TOKENS, D)[:, order_pos]
    return (block_out, input_grad, param_grad, new_params, new_moment1, new_moment2)
```

```python
import math

import jax
import jax.numpy as jnp
from jax import lax
from jax.sharding import PartitionSpec as P

D = 896
QUERY_HEADS = 14
KEY_VALUE_HEADS = 2
HEAD_SIZE = 64
FF = 4864
QW = 896
KEY_FEATURES = 128


theta_base = 1000000.0
norm_eps = 1e-06
beta_one = 0.9
beta_two = 0.95
adam_eps = 1e-08
learn_rate = 0.02
decay_rate = 0.1
step_count = 10.0


def piece_shapes():
    return [
        (D, 0),
        (D, QW),
        (QW, 0),
        (D, KEY_FEATURES),
        (KEY_FEATURES, 0),
        (D, KEY_FEATURES),
        (KEY_FEATURES, 0),
        (QW, D),
        (D, 0),
        (FF, D),
        (FF, D),
        (FF, D),
    ]


def shard_bounds(parts):
    bounds = [0]
    for rows_full, cols in piece_shapes():
        length = rows_full // parts
        if cols > 0:
            length = length * cols
        bounds.append(bounds[-1] + length)
    return bounds


def unpack(rows_arr, parts, first, last):
    bounds = shard_bounds(parts)
    shapes = piece_shapes()
    count = rows_arr.shape[0]
    base = bounds[first]
    result = []
    for number in range(first, last):
        rows_full, cols = shapes[number]
        piece = rows_arr[:, bounds[number] - base : bounds[number + 1] - base]
        if cols > 0:
            result.append(piece.reshape(count * (rows_full // parts), cols))
        else:
            result.append(piece.reshape(-1))
    return result


def decay_mask(index_vec, parts):
    bounds = shard_bounds(parts)
    result = jnp.zeros(index_vec.shape, jnp.float32)
    for number in (1, 3, 5, 7, 9, 10, 11):
        inside = (index_vec >= bounds[number]) & (index_vec < bounds[number + 1])
        result = result + jnp.where(inside, 1.0, 0.0).astype(jnp.float32)
    return result


def rope_tables(position):
    freq_index = jnp.arange(HEAD_SIZE // 2, dtype=jnp.float32)
    inverse = jnp.exp(freq_index * (-2.0 * math.log(theta_base) / HEAD_SIZE))
    angles = position.astype(jnp.float32)[:, None] * inverse[None, :]
    cosine_table = jnp.cos(angles)
    sine_lookup = jnp.sin(angles)
    return (
        jnp.concatenate([cosine_table, cosine_table], 1),
        jnp.concatenate([sine_lookup, sine_lookup], 1),
    )


def rotary_apply(values, cosine_table, sine_lookup):
    top_half = values[..., HEAD_SIZE // 2 :]
    low_half = values[..., : HEAD_SIZE // 2]
    turned = jnp.concatenate([-top_half, low_half], -1)
    return values * cosine_table[:, None, :] + turned * sine_lookup[:, None, :]


def rotary_inverse(gradient, cosine_table, sine_lookup):
    scaled = gradient * sine_lookup[:, None, :]
    turned = jnp.concatenate([scaled[..., HEAD_SIZE // 2 :], -scaled[..., : HEAD_SIZE // 2]], -1)
    return gradient * cosine_table[:, None, :] + turned


def lookup(table, index_vec):
    slots = jnp.arange(table.shape[0], dtype=jnp.int32)
    return jnp.sum(jnp.where(index_vec[..., None] == slots, table, 0), -1)


def outer_dot(left, right):
    return lax.dot_general(
        left, right, (((0,), (0,)), ((), ())), preferred_element_type=jnp.float32
    )


def inner_dot(left, right):
    return lax.dot_general(
        left, right, (((1,), (1,)), ((), ())), preferred_element_type=jnp.float32
    )


def gate_terms(gate_pre, up_pre, d_hidden):
    sigmoid_gate = jax.nn.sigmoid(gate_pre)
    silu_gate = gate_pre * sigmoid_gate
    d_gate = (d_hidden * up_pre * sigmoid_gate * (1.0 + gate_pre * (1.0 - sigmoid_gate))).astype(
        jnp.bfloat16
    )
    d_up = (d_hidden * silu_gate).astype(jnp.bfloat16)
    return (d_gate, d_up)


def hidden_units(gate_pre, up_pre):
    return (gate_pre * jax.nn.sigmoid(gate_pre) * up_pre).astype(jnp.bfloat16)


def body(block_in, cotangent, pairs, positions, params, moment1, moment2):
    n_ctx = lax.axis_size("ctx")
    n_wt = lax.axis_size("wt")
    token_rows = block_in.shape[1]
    half_rows = token_rows // 2
    seq_len = token_rows * n_ctx
    key_tile = min(512, seq_len)
    query_group_width = QUERY_HEADS // KEY_VALUE_HEADS
    score_scale = 1.0 / math.sqrt(HEAD_SIZE)
    ctx_id = lax.axis_index("ctx")
    wt_id = lax.axis_index("wt")
    x_rows = block_in[0]
    cot_rows = cotangent[0]
    row_bf = params.astype(jnp.bfloat16)
    prefix = shard_bounds(n_wt)[9]
    g1_s, wq_s, bq_s, wk_s, bk_s, wv_s, bv_s, wo_s, g2_s = unpack(row_bf[:, :prefix], n_wt, 0, 9)
    shard_rows = D // n_wt
    wide = 2 * QW + 2 * KEY_FEATURES
    vec = jnp.concatenate([g1_s, bq_s, bk_s, bv_s, g2_s])
    vec_rows = jnp.pad(vec.reshape(1, -1), ((0, 15), (0, wide - vec.shape[0])))
    attn_own = jnp.concatenate(
        [jnp.concatenate([wq_s, wo_s, wk_s, wv_s], 1), vec_rows], 0
    )
    attn_all = lax.all_gather(attn_own, "wt", axis=0, tiled=False)
    mats = attn_all[:, :shard_rows].reshape(D, wide)
    wq_b = mats[:, :QW]
    wo_b = mats[:, QW : 2 * QW]
    wk_b = mats[:, 2 * QW : 2 * QW + KEY_FEATURES]
    wv_b = mats[:, 2 * QW + KEY_FEATURES :]
    vecs = attn_all[:, shard_rows]
    vec_parts = []
    vec_at = 0
    for own in (g1_s, bq_s, bk_s, bv_s, g2_s):
        vec_parts.append(vecs[:, vec_at : vec_at + own.shape[0]].reshape(-1))
        vec_at += own.shape[0]
    gain_b, bq_b, bk_b, bv_b, gain_two = vec_parts
    gain_full = gain_b.astype(jnp.float32)
    inv_rms = lax.rsqrt(jnp.mean(x_rows * x_rows, -1, keepdims=True) + norm_eps)
    normed = (x_rows * inv_rms * gain_full).astype(jnp.bfloat16)
    queries = jnp.dot(normed, wq_b, preferred_element_type=jnp.float32) + bq_b.astype(jnp.float32)
    key_projected = jnp.dot(normed, wk_b, preferred_element_type=jnp.float32) + bk_b.astype(
        jnp.float32
    )
    value_projected = jnp.dot(normed, wv_b, preferred_element_type=jnp.float32) + bv_b.astype(
        jnp.float32
    )
    cosine_table, sine_lookup = rope_tables(positions[0])
    query_narrow = rotary_apply(
        queries.reshape(token_rows, QUERY_HEADS, HEAD_SIZE), cosine_table, sine_lookup
    ).astype(jnp.bfloat16)
    key_narrow = rotary_apply(
        key_projected.reshape(token_rows, KEY_VALUE_HEADS, HEAD_SIZE), cosine_table, sine_lookup
    ).astype(jnp.bfloat16)
    value_narrow = value_projected.astype(jnp.bfloat16)
    own_kv = jnp.concatenate([key_narrow.reshape(token_rows, KEY_FEATURES), value_narrow], 1)
    all_kv = lax.all_gather(own_kv, "ctx", axis=0, tiled=True)
    block_ids = jnp.arange(2 * n_ctx, dtype=jnp.int32)
    target = jnp.where(block_ids < n_ctx, block_ids, 2 * n_ctx - 1 - block_ids)
    owner = jnp.sum(
        jnp.where(
            pairs[None, :] == target[:, None], jnp.arange(n_ctx, dtype=jnp.int32)[None, :], 0
        ),
        1,
    )
    late_side = (block_ids >= n_ctx).astype(jnp.int32)
    causal_ids = jnp.arange(seq_len, dtype=jnp.int32)
    block_of = causal_ids // half_rows
    source_row = (
        lookup(owner, block_of) * token_rows
        + lookup(late_side, block_of) * half_rows
        + causal_ids % half_rows
    )
    sorted_kv = jnp.take(all_kv, source_row, axis=0)
    early_block = lookup(pairs, ctx_id)
    late_block = 2 * n_ctx - 1 - early_block

    def query_positions(block_now):
        return block_now * half_rows + jnp.arange(half_rows, dtype=jnp.int32)

    def tile_total(block_now):
        return ((block_now + 1) * half_rows + key_tile - 1) // key_tile

    def key_slice(tile_no):
        tile_start = tile_no * key_tile
        key_value_tile = lax.dynamic_slice_in_dim(sorted_kv, tile_start, key_tile, 0)
        key_block_tile = key_value_tile[:, :KEY_FEATURES].reshape(
            key_tile, KEY_VALUE_HEADS, HEAD_SIZE
        )
        value_tile = key_value_tile[:, KEY_FEATURES:].reshape(key_tile, KEY_VALUE_HEADS, HEAD_SIZE)
        k_pos = tile_start + jnp.arange(key_tile, dtype=jnp.int32)
        return (tile_start, key_block_tile, value_tile, k_pos)

    def attend(query_half, block_now):
        q_pos = query_positions(block_now)
        query_group = query_half.reshape(half_rows, KEY_VALUE_HEADS, query_group_width, HEAD_SIZE)

        def tile_scores(tile_no):
            tile_start, key_block_tile, value_tile, k_pos = key_slice(tile_no)
            scores = score_scale * jnp.einsum(
                "qkgd,tkd->kgqt", query_group, key_block_tile, preferred_element_type=jnp.float32
            )
            visible = k_pos[None, :] <= q_pos[:, None]
            return (jnp.where(visible, scores, -jnp.inf), value_tile)

        def total_step(tile_no, state_carry):
            run_peak, run_total = state_carry
            scores, value_tile = tile_scores(tile_no)
            new_peak = jnp.maximum(run_peak, jnp.max(scores, -1))
            factor = jnp.exp(run_peak - new_peak)
            run_total = run_total * factor + jnp.sum(jnp.exp(scores - new_peak[..., None]), -1)
            return (new_peak, run_total)

        tile_count = tile_total(block_now)
        initial_state = (
            jnp.full((KEY_VALUE_HEADS, query_group_width, half_rows), -jnp.inf, jnp.float32),
            jnp.zeros((KEY_VALUE_HEADS, query_group_width, half_rows), jnp.float32),
        )
        run_peak, run_total = lax.fori_loop(0, tile_count, total_step, initial_state)
        log_total = run_peak + jnp.log(run_total)

        def value_step(tile_no, run_accum):
            scores, value_tile = tile_scores(tile_no)
            prob_bf = jnp.exp(scores - log_total[..., None]).astype(jnp.bfloat16)
            return run_accum + jnp.einsum(
                "kgqt,tkd->kgqd", prob_bf, value_tile, preferred_element_type=jnp.float32
            )

        run_accum = lax.fori_loop(
            0,
            tile_count,
            value_step,
            jnp.zeros((KEY_VALUE_HEADS, query_group_width, half_rows, HEAD_SIZE), jnp.float32),
        )
        context_half = jnp.transpose(run_accum, (2, 0, 1, 3)).reshape(half_rows, QW)
        return (context_half, log_total)

    query_flat = query_narrow.reshape(token_rows, QW)
    ctx_early, lse_early = attend(query_flat[:half_rows], early_block)
    ctx_late, lse_late = attend(query_flat[half_rows:], late_block)
    context_rows = jnp.concatenate([ctx_early, ctx_late], 0)
    context_bf = context_rows.astype(jnp.bfloat16)
    feature_cols, context_cols = (
        lax.all_to_all(normed, "wt", split_axis=1, concat_axis=0, tiled=True),
        lax.all_to_all(context_bf, "wt", split_axis=1, concat_axis=0, tiled=True),
    )
    mid_rows = x_rows + jnp.dot(context_bf, wo_b, preferred_element_type=jnp.float32)
    gain_two_full = gain_two.astype(jnp.float32)
    inv_rms_two = lax.rsqrt(jnp.mean(mid_rows * mid_rows, -1, keepdims=True) + norm_eps)
    normed_two = (mid_rows * inv_rms_two * gain_two_full).astype(jnp.bfloat16)
    cot_bf = cot_rows.astype(jnp.bfloat16)
    pair_group = lax.all_gather(
        jnp.concatenate([normed_two, cot_bf], 1), "wt", axis=0, tiled=True
    )
    normed_group = pair_group[:, :D]
    cot_group = pair_group[:, D:]
    ff_own = row_bf[0, prefix:].reshape(3 * (FF // n_wt), D)
    wg_own, wu_own, wd_own = jnp.split(ff_own, 3, 0)
    gate_pre = inner_dot(normed_group, wg_own)
    up_pre = inner_dot(normed_group, wu_own)
    hidden_bf = hidden_units(gate_pre, up_pre)
    ff_sum = lax.psum_scatter(
        jnp.dot(hidden_bf, wd_own, preferred_element_type=jnp.float32),
        "wt",
        scatter_dimension=0,
        tiled=True,
    )
    d_hidden = inner_dot(cot_group, wd_own)
    d_gate, d_up = gate_terms(gate_pre, up_pre, d_hidden)
    grad_wg = outer_dot(d_gate, normed_group)
    grad_wu = outer_dot(d_up, normed_group)
    grad_wd = outer_dot(hidden_bf, cot_group)
    d_norm_two = lax.psum_scatter(
        jnp.dot(d_gate, wg_own, preferred_element_type=jnp.float32)
        + jnp.dot(d_up, wu_own, preferred_element_type=jnp.float32),
        "wt",
        scatter_dimension=0,
        tiled=True,
    )
    block_out = mid_rows + ff_sum
    grad_gain_two = jnp.sum(d_norm_two * mid_rows * inv_rms_two, 0)
    d_scaled_two = d_norm_two * gain_two_full
    d_mid = (
        cot_rows
        + inv_rms_two * d_scaled_two
        - mid_rows
        * (inv_rms_two * inv_rms_two * inv_rms_two)
        * jnp.mean(d_scaled_two * mid_rows, -1, keepdims=True)
    )
    d_mid_bf = d_mid.astype(jnp.bfloat16)
    context_gradient = inner_dot(d_mid_bf, wo_b)
    context_gradient_narrow = context_gradient.astype(jnp.bfloat16)
    delta_rows = jnp.sum(
        (context_gradient * context_rows).reshape(
            token_rows, KEY_VALUE_HEADS, query_group_width, HEAD_SIZE
        ),
        -1,
    )

    def attend_back(query_half, half_gradient, lse_half, delta_half, block_now, key_gradients):
        q_pos = query_positions(block_now)
        query_group = query_half.reshape(half_rows, KEY_VALUE_HEADS, query_group_width, HEAD_SIZE)
        group_gradient = half_gradient.reshape(
            half_rows, KEY_VALUE_HEADS, query_group_width, HEAD_SIZE
        )
        delta_t = jnp.transpose(delta_half, (1, 2, 0))[..., None]

        def tile_step(tile_no, state_carry):
            d_query, key_gradients = state_carry
            tile_start, key_block_tile, value_tile, k_pos = key_slice(tile_no)
            scores = score_scale * jnp.einsum(
                "qkgd,tkd->kgqt", query_group, key_block_tile, preferred_element_type=jnp.float32
            )
            visible = k_pos[None, :] <= q_pos[:, None]
            scores = jnp.where(visible, scores, -jnp.inf)
            prob_tile = jnp.where(visible, jnp.exp(scores - lse_half[..., None]), 0.0)
            prob_bf = prob_tile.astype(jnp.bfloat16)
            d_probs = jnp.einsum(
                "qkgd,tkd->kgqt", group_gradient, value_tile, preferred_element_type=jnp.float32
            )
            d_scores = (prob_tile * (d_probs - delta_t)).astype(jnp.bfloat16)
            d_query = d_query + score_scale * jnp.einsum(
                "kgqt,tkd->qkgd", d_scores, key_block_tile, preferred_element_type=jnp.float32
            )
            key_part = score_scale * jnp.einsum(
                "kgqt,qkgd->tkd", d_scores, query_group, preferred_element_type=jnp.float32
            )
            value_part = jnp.einsum(
                "kgqt,qkgd->tkd", prob_bf, group_gradient, preferred_element_type=jnp.float32
            )
            update = jnp.concatenate(
                [
                    key_part.reshape(key_tile, KEY_FEATURES),
                    value_part.reshape(key_tile, KEY_FEATURES),
                ],
                1,
            )
            current = lax.dynamic_slice_in_dim(key_gradients, tile_start, key_tile, 0)
            key_gradients = lax.dynamic_update_slice_in_dim(
                key_gradients, current + update, tile_start, 0
            )
            return (d_query, key_gradients)

        initial_state = (
            jnp.zeros((half_rows, KEY_VALUE_HEADS, query_group_width, HEAD_SIZE), jnp.float32),
            key_gradients,
        )
        return lax.fori_loop(0, tile_total(block_now), tile_step, initial_state)

    key_gradients = jnp.zeros((seq_len, 2 * KEY_FEATURES), jnp.float32)
    dq_early, key_gradients = attend_back(
        query_flat[:half_rows],
        context_gradient_narrow[:half_rows],
        lse_early,
        delta_rows[:half_rows],
        early_block,
        key_gradients,
    )
    dq_late, key_gradients = attend_back(
        query_flat[half_rows:],
        context_gradient_narrow[half_rows:],
        lse_late,
        delta_rows[half_rows:],
        late_block,
        key_gradients,
    )
    d_query_rot = jnp.concatenate([dq_early, dq_late], 0).reshape(
        token_rows, QUERY_HEADS, HEAD_SIZE
    )
    d_query = rotary_inverse(d_query_rot, cosine_table, sine_lookup).reshape(token_rows, QW)
    row_ids = jnp.arange(seq_len, dtype=jnp.int32)
    local_ids = row_ids % token_rows
    chosen = lookup(pairs, row_ids // token_rows)
    back_block = jnp.where(local_ids < half_rows, chosen, 2 * n_ctx - 1 - chosen)
    back_index = back_block * half_rows + local_ids % half_rows
    per_device = jnp.take(key_gradients, back_index, axis=0)
    owned_gradients = lax.psum_scatter(per_device, "ctx", scatter_dimension=0, tiled=True)
    key_gradient = rotary_inverse(
        owned_gradients[:, :KEY_FEATURES].reshape(token_rows, KEY_VALUE_HEADS, HEAD_SIZE),
        cosine_table,
        sine_lookup,
    ).reshape(token_rows, KEY_FEATURES)
    value_gradient = owned_gradients[:, KEY_FEATURES:]
    dq_bf = d_query.astype(jnp.bfloat16)
    dk_bf = key_gradient.astype(jnp.bfloat16)
    dv_bf = value_gradient.astype(jnp.bfloat16)
    d_norm = inner_dot(dq_bf, wq_b) + inner_dot(dk_bf, wk_b) + inner_dot(dv_bf, wv_b)
    grad_gain = jnp.sum(d_norm * x_rows * inv_rms, 0)
    d_scaled = d_norm * gain_full
    d_input = inv_rms * d_scaled - x_rows * (inv_rms * inv_rms * inv_rms) * jnp.mean(
        d_scaled * x_rows, -1, keepdims=True
    )
    input_grad = d_mid + d_input
    back_group = lax.all_gather(
        jnp.concatenate([d_mid_bf, dq_bf, dk_bf, dv_bf], 1), "wt", axis=0, tiled=True
    )
    mid_group = back_group[:, :D]
    query_grads = back_group[:, D : D + QW]
    key_grads_group = back_group[:, D + QW : D + QW + KEY_FEATURES]
    value_grads_group = back_group[:, D + QW + KEY_FEATURES :]
    gain_part, gain_two_part = (
        lax.psum_scatter(grad_gain, "wt", scatter_dimension=0, tiled=True),
        lax.psum_scatter(grad_gain_two, "wt", scatter_dimension=0, tiled=True),
    )
    grad_wq = outer_dot(feature_cols, query_grads)
    grad_wk = outer_dot(feature_cols, key_grads_group)
    grad_wv = outer_dot(feature_cols, value_grads_group)
    grad_wo = outer_dot(context_cols, mid_group)
    query_part = QW // n_wt
    key_part_len = KEY_FEATURES // n_wt
    bias_q = lax.dynamic_slice_in_dim(
        jnp.sum(query_grads.astype(jnp.float32), 0), wt_id * query_part, query_part, 0
    )
    bias_k = lax.dynamic_slice_in_dim(
        jnp.sum(key_grads_group.astype(jnp.float32), 0), wt_id * key_part_len, key_part_len, 0
    )
    bias_v = lax.dynamic_slice_in_dim(
        jnp.sum(value_grads_group.astype(jnp.float32), 0), wt_id * key_part_len, key_part_len, 0
    )
    piece_len = moment1.shape[1]
    piece_rows = -(-piece_len // D)
    pad_rows = -(-piece_rows // 32) * 32
    head_pieces = -(-prefix // piece_len)
    ff_grad = jnp.concatenate(
        [grad_wg, grad_wu, grad_wd, jnp.zeros((16, D), jnp.float32)], 0
    )
    spill = head_pieces * piece_len - prefix
    spill_rows = -(-spill // D)
    head = jnp.concatenate(
        [
            gain_part,
            grad_wq.reshape(-1),
            bias_q,
            grad_wk.reshape(-1),
            bias_k,
            grad_wv.reshape(-1),
            bias_v,
            grad_wo.reshape(-1),
            gain_two_part,
            ff_grad[:spill_rows].reshape(-1)[:spill],
        ]
    )
    laid = []
    for number in range(n_ctx):
        start = number * piece_len
        if number < head_pieces:
            flat = jnp.pad(head[start : start + piece_len], (0, piece_rows * D - piece_len))
            rows = flat.reshape(piece_rows, D)
        else:
            row_at, col_at = divmod(start - prefix, D)
            rows = ff_grad[row_at : row_at + piece_rows]
            if col_at:
                after = ff_grad[row_at + 1 : row_at + 1 + piece_rows, :col_at]
                rows = jnp.concatenate([rows[:, col_at:], after], 1)
        laid.append(jnp.pad(rows.astype(jnp.bfloat16), ((0, pad_rows - piece_rows), (0, 0))))
    own_rows = lax.psum_scatter(
        jnp.concatenate(laid, 0), "ctx", scatter_dimension=0, tiled=True
    )
    grad_piece = own_rows.astype(jnp.float32).reshape(-1)[:piece_len]
    param_grad = grad_piece.reshape(1, piece_len)
    piece_start = ctx_id * piece_len
    own_params = lax.dynamic_slice_in_dim(params[0], piece_start, piece_len, 0).reshape(
        1, piece_len
    )
    decay = decay_mask(piece_start + jnp.arange(piece_len, dtype=jnp.int32), n_wt).reshape(
        1, piece_len
    )
    new_moment1 = beta_one * moment1 + (1.0 - beta_one) * param_grad
    new_moment2 = beta_two * moment2 + (1.0 - beta_two) * param_grad * param_grad
    m_hat = new_moment1 / (1.0 - beta_one**step_count)
    v_hat = new_moment2 / (1.0 - beta_two**step_count)
    new_params = own_params - learn_rate * (
        m_hat / (jnp.sqrt(v_hat) + adam_eps) + decay_rate * decay * own_params
    )
    return (
        block_out.reshape(1, token_rows, D),
        input_grad.reshape(1, token_rows, D),
        param_grad,
        new_params,
        new_moment1,
        new_moment2,
    )


def solution(mesh):
    in_specs = (
        P("wt", "ctx", None),
        P("wt", "ctx", None),
        P(),
        P("wt", "ctx"),
        P("wt", None),
        P("wt", "ctx"),
        P("wt", "ctx"),
    )
    out_specs = (
        P("wt", "ctx", None),
        P("wt", "ctx", None),
        P("wt", "ctx"),
        P("wt", "ctx"),
        P("wt", "ctx"),
        P("wt", "ctx"),
    )
    return jax.shard_map(body, mesh=mesh, in_specs=in_specs, out_specs=out_specs, check_vma=False)
```
